32 devices in a mesh: dp: 2 (over core), pipe: 2 (over y), seq: 8 (over z, x).
Axes of the slice: x: 2, y: 2, z: 4, core: 2. Of those that a mesh axis runs over, the one named last changes fastest.
Arguments:
- slides_in: bfloat16 [4, 1024, 768], P('dp', 'seq'), may hold values from -6 to 6
- norm_gains: float32 [2, 2, 768], P('pipe'), may hold values from 0.1 to 1.9
- w_qkv: bfloat16 [2, 768, 2304], P('pipe', 'dp'), may hold values from -0.21875 to 0.21875
- w_out: bfloat16 [2, 768, 768], P('pipe', 'dp'), may hold values from -0.21875 to 0.21875
- w_up: bfloat16 [2, 768, 3072], P('pipe', 'dp'), may hold values from -0.21875 to 0.21875
- w_down: bfloat16 [2, 3072, 768], P('pipe', 'dp'), may hold values from -0.109375 to 0.109375
- key_owner: int32 [8, 12, 3], replicated, may hold values from 0 to 7, all different within a row; in each aligned block of 12 rows (0 to 11, 12 to 23, ..., all dimensions but the last counted through in order) at most 6 rows name the same one
- keep: int32 [4, 2], P('dp', 'pipe'), may hold values 0 or 1
Outputs:
- section_out: bfloat16 [2, 4, 1024, 768], P('pipe', 'dp', 'seq')
The draws below stay inside these ranges and needn't reach their ends.
Inputs may be any that keep to these rules, and one draw needn't show every extreme that they name: `key_owner`: each row names 3 different seq indices; among the rows of one index of seq no seq index is named more than 6 times.
All inputs are finite; a program needn't handle non-finite values. No bound on the sum of `keep` on one device may be relied on, other than what follows from the above.
Results may differ from the reference program's by a relative error of at most 0.015.
Values may be sent and summed in bfloat16 or wider, within the bound.
A program may use at most 128 MiB of HBM per device.

```python
import math
import jax
import jax.numpy as jnp
import numpy as np
from jax import lax

D = 768
H = 12
HD = 64
FF = 3072
BLOCK = 128
NSEL = 4
LAY = 1
BLK_DEV = 1
NBLK = 8
TOKENS = 1024
SLIDES = 4
LAYERS = 2
CAP = 6
N_SEQ = 8


def plant(drawn, own_key, low, largest):
    dims = drawn.shape
    spot = [jax.random.randint(jax.random.fold_in(own_key, axis), (), 0, dims[axis]) for axis in range(len(dims))]
    drawn = drawn.at[tuple(spot)].set(low)
    longest = dims.index(max(dims))
    spot[longest] = (spot[longest] + 1) % dims[longest]
    return drawn.at[tuple(spot)].set(largest)


def block_scale(key, extent, cuts, smallest, largest):
    def one(dim, parts):
        steps = jax.random.uniform(jax.random.fold_in(jax.random.fold_in(key, 6), dim), (parts,), jnp.float32, smallest / len(cuts), largest / len(cuts))
        return jnp.repeat(jnp.exp(steps), extent[dim] // parts).reshape((-1,) + (1,) * (len(extent) - dim - 1))

    factor_of = one(*cuts[0])
    for cut in cuts[1:]:
        factor_of = factor_of * one(*cut)
    return factor_of


def routed_block(key, own, number, rows, amount, top, bound, skew):
    sequence = jax.random.permutation(key, amount)
    packed, usual = load_shares(amount, rows * top, bound, skew, True), load_shares(amount, rows * top, bound, skew, False)
    places = jnp.arange(amount)

    def named(lengths, offset_by):
        used = int((lengths > 0).sum())
        fixed = max(1, used // 4)
        moved = fixed + (places - fixed + offset_by * (used - fixed)) % max(1, amount - fixed)
        return jnp.zeros((amount,), jnp.int32).at[sequence[jnp.where(places < fixed, places, moved)]].set(jnp.asarray(lengths, jnp.int32))

    lengths = jnp.where(number % 4 == 0, named(packed, number // 4), named(usual, number - number // 4 - 1))
    mixed = jax.random.permutation(jax.random.fold_in(own, 3), amount)
    giver, taker = mixed[0:amount // 2 * 2:2], mixed[1:amount // 2 * 2:2]
    room = jnp.minimum(lengths[giver] - 1, bound - lengths[taker]) // 2
    room = jnp.where((giver == sequence[0]) | (taker == sequence[0]) | (lengths[taker] == 0), 0, jnp.maximum(room, 0))
    moved = jax.random.randint(jax.random.fold_in(own, 4), (amount // 2,), 0, 1 << 20) % (room + 1)
    lengths = lengths.at[giver].add(-moved).at[taker].add(moved)
    items = jnp.searchsorted(jnp.cumsum(lengths), jnp.arange(rows * top), side="right").astype(jnp.int32)
    table = items.reshape(top, rows).T
    table = table[jax.random.permutation(jax.random.fold_in(own, 1), rows)]
    offset_by = jax.random.randint(jax.random.fold_in(own, 2), (rows, 1), 0, top)
    return jnp.take_along_axis(table, (jnp.arange(top)[None, :] + offset_by) % top, axis=1)


def load_shares(amount, total, limit, skew, full):
    loads = [(1 << 20) // math.isqrt(grade ** skew) + 1 for grade in range(1, amount + 1)]
    largest = limit if full else min(limit, max(-(-total // amount), total * loads[0] // sum(loads)))
    least = 1 if total - largest >= amount - 1 else 0
    holding, rest = [largest] + [least] * (amount - 1), total - largest - least * (amount - 1)
    while rest > 0:
        free = [i for i in range(1, amount) if holding[i] < largest] or [i for i in range(1, amount) if holding[i] < limit]
        whole, remaining = sum([loads[i] for i in free]), rest
        for i in free:
            more = min(limit - holding[i], max(1, remaining * loads[i] // whole), rest)
            holding[i] = holding[i] + more
            rest = rest - more
    return np.array(holding)


def bell_draw(stream_key, shape, deviation, bound, cuts=(), kind=jnp.bfloat16):
    drawn = deviation * jax.random.normal(stream_key, shape, jnp.float32)
    if cuts:
        drawn = drawn * block_scale(stream_key, shape, cuts, -0.22, 0.18)
    return jnp.clip(drawn, -bound, bound).astype(kind)


def setup_inputs(seed: int = 0) -> dict:
    seeds = jax.random.split(jax.random.key(seed), 9)
    slides_in = bell_draw(seeds[0], (SLIDES, TOKENS, D), 1.0, 6.0, ((0, 2), (1, 8)))
    norm_gains = jnp.clip(1.0 + 0.18 * jax.random.normal(seeds[1], (LAYERS, 2, D), jnp.float32), 0.1, 1.9)
    w_qkv = bell_draw(seeds[2], (LAYERS, D, 3 * D), D ** -0.5, 0.21875, ((0, 2), (1, 2)))
    w_out = bell_draw(seeds[3], (LAYERS, D, D), D ** -0.5, 0.21875, ((0, 2), (1, 2)))
    w_up = bell_draw(seeds[4], (LAYERS, D, FF), D ** -0.5, 0.21875, ((0, 2), (1, 2)))
    w_down = bell_draw(seeds[5], (LAYERS, FF, D), FF ** -0.5, 0.109375, ((0, 2), (1, 2)))
    key_owner_keys = jax.random.split(jax.random.fold_in(seeds[6], 1), NBLK * H // (BLK_DEV * H))
    key_owner_turns = jax.random.permutation(jax.random.fold_in(seeds[6], 3), NBLK * H // (BLK_DEV * H))
    key_owner = jax.vmap(lambda own, number: routed_block(jax.random.fold_in(seeds[6], 2), own, number, BLK_DEV * H, N_SEQ, NSEL - 1, CAP, 2))(key_owner_keys, key_owner_turns).reshape((NBLK, H, NSEL - 1))
    keep = plant((jax.random.randint(seeds[7], (SLIDES, LAYERS), 0, 4) < 3).astype(jnp.int32), jax.random.fold_in(seeds[7], 1), 0, 1)
    return dict(slides_in=slides_in, norm_gains=norm_gains, w_qkv=w_qkv, w_out=w_out, w_up=w_up, w_down=w_down, key_owner=key_owner, keep=keep)


def layer_norm(values, gain):
    mean = lax.optimization_barrier(jnp.mean(values, axis=-1, keepdims=True))
    centred = values - mean
    var = lax.optimization_barrier(jnp.mean(centred * centred, axis=-1, keepdims=True))
    return centred * lax.rsqrt(var + 1e-05) * gain

def one_layer(x, gains, wqkv, wout, wup, wdown, key_index, flag):
    n1 = layer_norm(x.astype(jnp.float32), gains[0]).astype(jnp.bfloat16)
    qkv = jnp.dot(n1, wqkv, preferred_element_type=jnp.float32).astype(jnp.bfloat16)
    query = qkv[:, :D].reshape(NBLK, BLOCK, H, HD)
    keys = qkv[:, D:2 * D].reshape(NBLK, BLOCK, H, HD).transpose(0, 2, 1, 3)
    vals = qkv[:, 2 * D:].reshape(NBLK, BLOCK, H, HD).transpose(0, 2, 1, 3)
    head_ids = jnp.arange(H, dtype=jnp.int32)[None, :, None]
    far_keys = keys[key_index, head_ids]
    far_vals = vals[key_index, head_ids]
    key_list = jnp.concatenate([keys[:, :, None], far_keys], axis=2).reshape(NBLK, H, NSEL * BLOCK, HD)
    val_list = jnp.concatenate([vals[:, :, None], far_vals], axis=2).reshape(NBLK, H, NSEL * BLOCK, HD)

    def attend(pieces):
        qblk, kblk, vblk = pieces
        scores = jnp.einsum('qhd,hkd->hqk', qblk.astype(jnp.float32), kblk.astype(jnp.float32)) * 0.125
        probs = jax.nn.softmax(scores, axis=-1).astype(jnp.bfloat16)
        ctx = jnp.einsum('hqk,hkd->qhd', probs.astype(jnp.float32), vblk.astype(jnp.float32))
        return ctx.astype(jnp.bfloat16)
    ctx = lax.map(attend, (query, key_list, val_list)).reshape(NBLK * BLOCK, D)
    flag_f = flag.astype(jnp.float32)
    branch = jnp.dot(ctx, wout, preferred_element_type=jnp.float32)
    hidden = (x.astype(jnp.float32) + flag_f * branch).astype(jnp.bfloat16)
    n2 = layer_norm(hidden.astype(jnp.float32), gains[1]).astype(jnp.bfloat16)
    upper = jnp.dot(n2, wup, preferred_element_type=jnp.float32)
    act = jax.nn.gelu(upper, approximate=True).astype(jnp.bfloat16)
    down = jnp.dot(act, wdown, preferred_element_type=jnp.float32)
    return (hidden.astype(jnp.float32) + flag_f * down).astype(jnp.bfloat16)

def reference(slides_in, norm_gains, w_qkv, w_out, w_up, w_down, key_owner, keep):
    own_slot = (jnp.arange(NBLK, dtype=jnp.int32) % BLK_DEV)[:, None, None]
    key_index = (key_owner * BLK_DEV + own_slot).astype(jnp.int32)
    results = []
    for slide in range(SLIDES):
        x = slides_in[slide]
        per_section = []
        for layer in range(LAYERS):
            x = one_layer(x, norm_gains[layer], w_qkv[layer], w_out[layer], w_up[layer], w_down[layer], key_index, keep[slide, layer])
            if (layer + 1) % LAY == 0:
                per_section.append(x)
        results.append(jnp.stack(per_section, axis=0))
    return jnp.stack(results, axis=1)
```

```python
import functools

import jax
import jax.numpy as jnp
from jax import lax
from jax.experimental import pallas as pl
from jax.experimental.pallas import tpu as pltpu
from jax.sharding import PartitionSpec as P

H = 12
HD = 64
BLOCK = 128
PICKS = 3
CHUNK = 512
PIECES = 4
GO = 1
MESH_ID = pl.DeviceIdType.MESH


def layer_norm(values, gain):
    mean = jnp.mean(values, axis=-1, keepdims=True)
    centred = values - mean
    var = jnp.mean(centred * centred, axis=-1, keepdims=True)
    return centred * lax.rsqrt(var + 1e-05) * gain


def kernel(
    peers, sections, micro, slides, gains, wqkv_h, wout_h, wup_h, wdown_h, owners_h, keep_h, out,
    xg, kv, wqkv, wout, wup, wdown, qbuf, ctx, hid, n2b, acc, xo, owners, keep,
    wl_sem, ws_sem, wr_sem, in_sem, out_sem, ps_sem, pr_sem,
    cw_s, cw_r, cc_s, cc_r, small_sem, go_sem,
):
    width = slides.shape[2]
    ff = wup_h.shape[2]
    half_ring = peers // 2
    core = lax.axis_index("dp")
    section = lax.axis_index("pipe")
    me = lax.axis_index("seq")

    def pos_of(i):
        z, x = i // 2, i % 2
        return z + x * (peers - 1 - 2 * z)

    def at_pos(p):
        p = (p + 2 * peers) % peers
        x = p // half_ring
        return 2 * (p + x * (peers - 1 - 2 * p)) + x

    pos = pos_of(me)
    right, left = at_pos(pos + 1), at_pos(pos - 1)
    partner = 1 - core
    after = (section + 1) % sections
    before = (section + sections - 1) % sections

    def own_copy(s):
        return pltpu.make_async_copy(slides.at[s], xg.at[s, me], in_sem.at[s])

    @pl.when(section == 0)
    def _():
        for s in range(micro):
            own_copy(s).start()

    pltpu.make_async_copy(owners_h, owners, small_sem.at[0]).start()
    pltpu.make_async_copy(keep_h, keep, small_sem.at[1]).start()

    halves = ((wqkv_h, wqkv), (wout_h, wout), (wup_h, wup), (wdown_h, wdown))

    def weight_local(i):
        part, full = halves[i]
        rows = part.shape[1]
        return pltpu.make_async_copy(
            part.at[0], full.at[pl.ds(pl.multiple_of(core * rows, rows), rows)], wl_sem.at[i]
        )

    def weight_remote(i, place):
        part, full = halves[i]
        rows = part.shape[1]
        return pltpu.make_async_remote_copy(
            src_ref=part.at[0],
            dst_ref=full.at[pl.ds(pl.multiple_of(place * rows, rows), rows)],
            send_sem=ws_sem.at[i],
            recv_sem=wr_sem.at[i],
            device_id={"dp": partner},
            device_id_type=MESH_ID,
        )

    for i in range(4):
        weight_local(i).start()

    barrier = pltpu.get_barrier_semaphore()
    for target in (
        {"dp": partner}, {"seq": left}, {"seq": right}, {"pipe": after}, {"pipe": before},
    ):
        pl.semaphore_signal(barrier, inc=1, device_id=target, device_id_type=MESH_ID)
    pl.semaphore_wait(barrier, 5)

    for i in range(4):
        weight_remote(i, core).start()

    rows_of = [pl.ds(c * (BLOCK // PIECES), BLOCK // PIECES) for c in range(PIECES)]

    def clockwise(s, k, c, owner):
        piece = xg.at[s, owner, rows_of[c]]
        return pltpu.make_async_remote_copy(
            src_ref=piece, dst_ref=piece, send_sem=cw_s.at[s, k, c], recv_sem=cw_r.at[s, k, c],
            device_id={"seq": right}, device_id_type=MESH_ID,
        )

    def counter(s, k, c, owner):
        piece = xg.at[s, owner, rows_of[c]]
        return pltpu.make_async_remote_copy(
            src_ref=piece, dst_ref=piece, send_sem=cc_s.at[s, k, c], recv_sem=cc_r.at[s, k, c],
            device_id={"seq": left}, device_id_type=MESH_ID,
        )

    def pass_on(s, c):
        return pltpu.make_async_remote_copy(
            src_ref=xo.at[s, rows_of[c]], dst_ref=xg.at[s, me, rows_of[c]],
            send_sem=ps_sem.at[s, c], recv_sem=pr_sem.at[s, c],
            device_id={"pipe": after}, device_id_type=MESH_ID,
        )

    order = list(zip(range(PIECES), reversed(range(PIECES))))

    def start_first(s):
        if s == 0:
            pl.when(core == 0)(lambda: own_copy(s).wait())
        else:
            own_copy(s).wait()
        for c, d in order:
            clockwise(s, 0, c, me).start()
            counter(s, 0, d, me).start()

    def start_passed(s):
        for c in range(PIECES):
            pass_on(s, c).wait_recv()
            clockwise(s, 0, c, me).start()
            counter(s, 0, c, me).start()

    def forward(s, k):
        a, b = at_pos(pos - k - 1), at_pos(pos + k + 1)
        for i, (c, d) in enumerate(order):
            clockwise(s, k, c, a).wait_recv()
            if i < PIECES // 2:
                clockwise(s, k + 1, c, a).start()
            else:
                pl.when(k < half_ring - 2)(lambda: clockwise(s, k + 1, c, a).start())
            counter(s, k, d, b).wait_recv()
            if i < PIECES // 2:
                counter(s, k + 1, d, b).start()
            else:
                pl.when(k < half_ring - 2)(lambda: counter(s, k + 1, d, b).start())

    gain1 = gains[0, 0:1, :]
    gain2 = gains[0, 1:2, :]

    def keys_values(blocks, n1):
        for c in range(0, 2 * width, CHUNK):
            part = jnp.dot(
                n1, wqkv[:, width + c : width + c + CHUNK], preferred_element_type=jnp.float32
            ).astype(jnp.bfloat16)
            for b, block in enumerate(blocks):
                kv[block, :, c : c + CHUNK] = part[b * BLOCK : (b + 1) * BLOCK]

    def gather(s):
        if s == 0:
            pl.when((section == 0) & (core == 1))(lambda: own_copy(0).wait())
        n1 = layer_norm(xg[s, me].astype(jnp.float32), gain1).astype(jnp.bfloat16)
        if s == 0:
            weight_local(0).wait()
            weight_remote(0, partner).wait_recv()
        qbuf[...] = jnp.dot(
            n1, wqkv[:, :width], preferred_element_type=jnp.float32
        ).astype(jnp.bfloat16)
        keys_values((me,), n1)

        if s == 0:
            @pl.when((section == 0) & (core == 1))
            def _():
                pl.semaphore_wait(go_sem, 1)
                start_first(0)

        def step(k, carry):
            if s == 0:
                forward(s, k)
                @pl.when((section == 0) & (core == 0) & (k == GO))
                def _():
                    pl.semaphore_signal(go_sem, inc=1, device_id={"dp": partner}, device_id_type=MESH_ID)
            else:
                pl.when(k >= 1)(lambda: forward(s, k))
            a, b = at_pos(pos - k - 1), at_pos(pos + k + 1)
            both = jnp.concatenate([xg[s, a], xg[s, b]], axis=0).astype(jnp.float32)
            keys_values((a, b), layer_norm(both, gain1).astype(jnp.bfloat16))
            return carry

        lax.fori_loop(0, half_ring - 1, step, 0)
        if s + 1 < micro:
            pl.when(section == 0)(lambda: start_first(s + 1))
        far = at_pos(pos + half_ring)
        for c, d in order[: PIECES // 2]:
            clockwise(s, half_ring - 1, c, far).wait_recv()
            counter(s, half_ring - 1, d, far).wait_recv()
        n1 = layer_norm(xg[s, far].astype(jnp.float32), gain1).astype(jnp.bfloat16)
        keys_values((far,), n1)

    lane = lax.broadcasted_iota(jnp.int32, (1, 2 * HD), 1)
    low = lane < HD
    low_mask = low.astype(jnp.float32).astype(jnp.bfloat16)
    high_mask = (lane >= HD).astype(jnp.float32).astype(jnp.bfloat16)

    def attend(s):
        def pair(j, carry):
            kcols = pl.ds(pl.multiple_of(j * 2 * HD, 2 * HD), 2 * HD)
            vcols = pl.ds(pl.multiple_of(width + j * 2 * HD, 2 * HD), 2 * HD)
            q = qbuf[:, kcols]
            results = []
            for e, mask in enumerate((low_mask, high_mask)):
                listed = [me] + [owners[i, me, 2 * j + e] for i in range(PICKS)]
                keys = jnp.concatenate([kv[o, :, kcols] for o in listed], axis=0)
                vals = jnp.concatenate([kv[o, :, vcols] for o in listed], axis=0)
                scores = lax.dot_general(
                    q * mask, keys, (((1,), (1,)), ((), ())), preferred_element_type=jnp.float32
                ) * 0.125
                top = jnp.max(scores, axis=-1, keepdims=True)
                probs = jnp.exp(scores - top)
                total = jnp.sum(probs, axis=-1, keepdims=True)
                res = jnp.dot(
                    probs.astype(jnp.bfloat16), vals, preferred_element_type=jnp.float32
                )
                results.append(res / total)
            ctx[:, kcols] = jnp.where(low, results[0], results[1]).astype(jnp.bfloat16)
            return carry

        lax.fori_loop(0, H // 2, pair, 0, unroll=True)

    def feed_forward(s):
        flag = keep[0, s].astype(jnp.float32)
        if s == 0:
            weight_local(1).wait()
            weight_remote(1, partner).wait_recv()
        branch = jnp.dot(ctx[...], wout[...], preferred_element_type=jnp.float32)
        hidden = (xg[s, me].astype(jnp.float32) + flag * branch).astype(jnp.bfloat16)
        hid[...] = hidden
        n2b[...] = layer_norm(hidden.astype(jnp.float32), gain2).astype(jnp.bfloat16)
        if s == 0:
            for i in (2, 3):
                weight_local(i).wait()
                weight_remote(i, partner).wait_recv()
        acc[...] = jnp.zeros_like(acc)

        def chunk(c, carry):
            cols = pl.ds(pl.multiple_of(c * CHUNK, CHUNK), CHUNK)
            upper = jnp.dot(n2b[...], wup[:, cols], preferred_element_type=jnp.float32)
            act = jax.nn.gelu(upper, approximate=True).astype(jnp.bfloat16)
            acc[...] += jnp.dot(act, wdown[cols, :], preferred_element_type=jnp.float32)
            return carry

        lax.fori_loop(0, 4, chunk, 0, unroll=True)
        if s == 0:
            forward(1, 0)
        lax.fori_loop(4, ff // CHUNK, chunk, 0, unroll=True)
        xo[s] = (hid[...].astype(jnp.float32) + flag * acc[...]).astype(jnp.bfloat16)

        @pl.when(section < sections - 1)
        def _():
            for c in range(PIECES):
                pass_on(s, c).start()

        pltpu.make_async_copy(xo.at[s], out.at[0, s], out_sem.at[s]).start()

    pltpu.make_async_copy(owners_h, owners, small_sem.at[0]).wait()
    pltpu.make_async_copy(keep_h, keep, small_sem.at[1]).wait()
    @pl.when((section == 0) & (core == 0))
    def _():
        start_first(0)
    pl.when(section > 0)(lambda: start_passed(0))
    for s in range(micro):
        gather(s)
        if s + 1 < micro:
            pl.when(section > 0)(lambda: start_passed(s + 1))
        attend(s)
        feed_forward(s)

    for s in range(micro):
        pltpu.make_async_copy(xo.at[s], out.at[0, s], out_sem.at[s]).wait()

        @pl.when(section < sections - 1)
        def _():
            for c in range(PIECES):
                pass_on(s, c).wait_send()

        def drain(k, carry):
            for c in range(PIECES):
                clockwise(s, k, c, at_pos(pos - k)).wait_send()
                counter(s, k, c, at_pos(pos + k)).wait_send()
            return carry

        lax.fori_loop(0, half_ring - 1, drain, 0)
        for c, d in order[: PIECES // 2]:
            clockwise(s, half_ring - 1, c, at_pos(pos - half_ring + 1)).wait_send()
            counter(s, half_ring - 1, d, at_pos(pos + half_ring - 1)).wait_send()
    for i in range(4):
        weight_remote(i, core).wait_send()


def per_device(peers, sections, slides, gains, wqkv, wout, wup, wdown, owners, keep):
    micro, rows, width = slides.shape
    owners, keep = jnp.transpose(owners, (2, 0, 1)), jnp.transpose(keep)
    ff = wup.shape[2]
    any_spec = pl.BlockSpec(memory_space=pl.ANY)
    bf16, f32 = jnp.bfloat16, jnp.float32
    dma = pltpu.SemaphoreType.DMA
    return pl.pallas_call(
        functools.partial(kernel, peers, sections, micro),
        out_shape=jax.ShapeDtypeStruct((1, micro, rows, width), bf16),
        in_specs=[
            any_spec, pl.BlockSpec(memory_space=pltpu.VMEM),
            any_spec, any_spec, any_spec, any_spec, any_spec, any_spec,
        ],
        out_specs=any_spec,
        scratch_shapes=[
            pltpu.VMEM((micro, peers, rows, width), bf16),
            pltpu.VMEM((peers, rows, 2 * width), bf16),
            pltpu.VMEM((width, 3 * width), bf16),
            pltpu.VMEM((width, width), bf16),
            pltpu.VMEM((width, ff), bf16),
            pltpu.VMEM((ff, width), bf16),
            pltpu.VMEM((rows, width), bf16),
            pltpu.VMEM((rows, width), bf16),
            pltpu.VMEM((rows, width), bf16),
            pltpu.VMEM((rows, width), bf16),
            pltpu.VMEM((rows, width), f32),
            pltpu.VMEM((micro, rows, width), bf16),
            pltpu.SMEM(owners.shape, jnp.int32),
            pltpu.SMEM(keep.shape, jnp.int32),
            dma((4,)), dma((4,)), dma((4,)),
            dma((micro,)), dma((micro,)), dma((micro, PIECES)), dma((micro, PIECES)),
            dma((micro, peers // 2, PIECES)), dma((micro, peers // 2, PIECES)),
            dma((micro, peers // 2, PIECES)), dma((micro, peers // 2, PIECES)),
            dma((2,)), pltpu.SemaphoreType.REGULAR,
        ],
        compiler_params=pltpu.CompilerParams(
            collective_id=0, has_side_effects=True, vmem_limit_bytes=60 * 1024 * 1024
        ),
    )(slides, gains, wqkv, wout, wup, wdown, owners, keep)


def solution(mesh):
    return jax.shard_map(
        functools.partial(per_device, mesh.shape["seq"], mesh.shape["pipe"]),
        mesh=mesh,
        in_specs=(
            P("dp", "seq", None),
            P("pipe", None, None),
            P("pipe", "dp", None),
            P("pipe", "dp", None),
            P("pipe", "dp", None),
            P("pipe", "dp", None),
            P(),
            P("dp", "pipe"),
        ),
        out_specs=P("pipe", "dp", "seq", None),
        check_vma=False,
    )
```

```python
import functools

import jax
import jax.numpy as jnp
from jax import lax
from jax.experimental import pallas as pl
from jax.experimental.pallas import tpu as pltpu
from jax.sharding import PartitionSpec as P

H = 12
HD = 64
BLOCK = 128
PICKS = 3
AHEAD = 2
CHUNK = 512
PIECES = 4
MESH_ID = pl.DeviceIdType.MESH


def layer_norm(values, gain):
    mean = jnp.mean(values, axis=-1, keepdims=True)
    centred = values - mean
    var = jnp.mean(centred * centred, axis=-1, keepdims=True)
    return centred * lax.rsqrt(var + 1e-05) * gain


def kernel(
    peers, sections, micro, slides, gains, wqkv_h, wout_h, wup_h, wdown_h, owners_h, keep_h, out,
    xg, kv, wqkv, wout, wup, wdown, qbuf, ctx, xo, owners, keep,
    wl_sem, ws_sem, wr_sem, in_sem, out_sem, ps_sem, pr_sem,
    cw_s, cw_r, cc_s, cc_r, small_sem,
):
    width = slides.shape[2]
    ff = wup_h.shape[2]
    half_ring = peers // 2
    core = lax.axis_index("dp")
    section = lax.axis_index("pipe")
    me = lax.axis_index("seq")

    def pos_of(i):
        z, x = i // 2, i % 2
        return z + x * (peers - 1 - 2 * z)

    def at_pos(p):
        p = (p + 2 * peers) % peers
        x = p // half_ring
        return 2 * (p + x * (peers - 1 - 2 * p)) + x

    pos = pos_of(me)
    right, left = at_pos(pos + 1), at_pos(pos - 1)
    partner = 1 - core
    after = (section + 1) % sections
    before = (section + sections - 1) % sections

    def own_copy(s):
        return pltpu.make_async_copy(slides.at[s], xg.at[s, me], in_sem.at[s])

    @pl.when(section == 0)
    def _():
        for s in range(micro):
            own_copy(s).start()

    pltpu.make_async_copy(owners_h, owners, small_sem.at[0]).start()
    pltpu.make_async_copy(keep_h, keep, small_sem.at[1]).start()

    halves = ((wqkv_h, wqkv), (wout_h, wout), (wup_h, wup), (wdown_h, wdown))

    def weight_local(i):
        part, full = halves[i]
        rows = part.shape[1]
        return pltpu.make_async_copy(
            part.at[0], full.at[pl.ds(pl.multiple_of(core * rows, rows), rows)], wl_sem.at[i]
        )

    def weight_remote(i, place):
        part, full = halves[i]
        rows = part.shape[1]
        return pltpu.make_async_remote_copy(
            src_ref=part.at[0],
            dst_ref=full.at[pl.ds(pl.multiple_of(place * rows, rows), rows)],
            send_sem=ws_sem.at[i],
            recv_sem=wr_sem.at[i],
            device_id={"dp": partner},
            device_id_type=MESH_ID,
        )

    for i in range(4):
        weight_local(i).start()

    barrier = pltpu.get_barrier_semaphore()
    for target in (
        {"dp": partner}, {"seq": left}, {"seq": right}, {"pipe": after}, {"pipe": before},
    ):
        pl.semaphore_signal(barrier, inc=1, device_id=target, device_id_type=MESH_ID)
    pl.semaphore_wait(barrier, 5)

    for i in range(4):
        weight_remote(i, core).start()

    rows_of = [pl.ds(c * (BLOCK // PIECES), BLOCK // PIECES) for c in range(PIECES)]

    def clockwise(s, k, c, owner):
        piece = xg.at[s, owner, rows_of[c]]
        return pltpu.make_async_remote_copy(
            src_ref=piece, dst_ref=piece, send_sem=cw_s.at[s, k, c], recv_sem=cw_r.at[s, k, c],
            device_id={"seq": right}, device_id_type=MESH_ID,
        )

    def counter(s, k, c, owner):
        piece = xg.at[s, owner, rows_of[c]]
        return pltpu.make_async_remote_copy(
            src_ref=piece, dst_ref=piece, send_sem=cc_s.at[s, k, c], recv_sem=cc_r.at[s, k, c],
            device_id={"seq": left}, device_id_type=MESH_ID,
        )

    def pass_on(s, c):
        return pltpu.make_async_remote_copy(
            src_ref=xo.at[s, rows_of[c]], dst_ref=xg.at[s, me, rows_of[c]],
            send_sem=ps_sem.at[s, c], recv_sem=pr_sem.at[s, c],
            device_id={"pipe": after}, device_id_type=MESH_ID,
        )

    order = list(zip(range(PIECES), reversed(range(PIECES))))

    def start_first(s):
        own_copy(s).wait()
        for c, d in order:
            clockwise(s, 0, c, me).start()
            counter(s, 0, d, me).start()

    def start_passed(s):
        for c in range(PIECES):
            pass_on(s, c).wait_recv()
            clockwise(s, 0, c, me).start()
            counter(s, 0, c, me).start()

    def forward(s, k):
        a, b = at_pos(pos - k - 1), at_pos(pos + k + 1)
        for i, (c, d) in enumerate(order):
            clockwise(s, k, c, a).wait_recv()
            if i < PIECES // 2:
                clockwise(s, k + 1, c, a).start()
            else:
                pl.when(k < half_ring - 2)(lambda: clockwise(s, k + 1, c, a).start())
            counter(s, k, d, b).wait_recv()
            if i < PIECES // 2:
                counter(s, k + 1, d, b).start()
            else:
                pl.when(k < half_ring - 2)(lambda: counter(s, k + 1, d, b).start())

    gain1 = gains[0, 0:1, :]
    gain2 = gains[0, 1:2, :]

    def keys_values(blocks, n1):
        for c in range(0, 2 * width, CHUNK):
            part = jnp.dot(
                n1, wqkv[:, width + c : width + c + CHUNK], preferred_element_type=jnp.float32
            ).astype(jnp.bfloat16)
            for b, block in enumerate(blocks):
                kv[block, :, c : c + CHUNK] = part[b * BLOCK : (b + 1) * BLOCK]

    def gather(s):
        n1 = layer_norm(xg[s, me].astype(jnp.float32), gain1).astype(jnp.bfloat16)
        if s == 0:
            weight_local(0).wait()
            weight_remote(0, partner).wait_recv()
        qbuf[...] = jnp.dot(
            n1, wqkv[:, :width], preferred_element_type=jnp.float32
        ).astype(jnp.bfloat16)
        keys_values((me,), n1)

        def step(k, carry):
            if s == 0:
                forward(s, k)
            else:
                pl.when(k >= 1)(lambda: forward(s, k))
            a, b = at_pos(pos - k - 1), at_pos(pos + k + 1)
            both = jnp.concatenate([xg[s, a], xg[s, b]], axis=0).astype(jnp.float32)
            keys_values((a, b), layer_norm(both, gain1).astype(jnp.bfloat16))
            return carry

        lax.fori_loop(0, half_ring - 1, step, 0)
        if s + 1 < micro:
            pl.when(section == 0)(lambda: start_first(s + 1))
        far = at_pos(pos + half_ring)
        for c, d in order[: PIECES // 2]:
            clockwise(s, half_ring - 1, c, far).wait_recv()
            counter(s, half_ring - 1, d, far).wait_recv()
        n1 = layer_norm(xg[s, far].astype(jnp.float32), gain1).astype(jnp.bfloat16)
        keys_values((far,), n1)

    lane = lax.broadcasted_iota(jnp.int32, (1, 2 * HD), 1)
    low = lane < HD
    masks = [
        jnp.where(low, 0.125, 0.0).astype(jnp.bfloat16),
        jnp.where(low, 0.0, 0.125).astype(jnp.bfloat16),
    ]

    def attend(s):
        def listed(h, base):
            cols = pl.ds(base + h // 2 * 2 * HD, 2 * HD)
            blocks = [me] + [owners[i, me, h] for i in range(PICKS)]
            return jnp.concatenate([kv[o, :, cols] for o in blocks], axis=0)

        def score(h):
            q = qbuf[:, pl.ds(h // 2 * 2 * HD, 2 * HD)] * masks[h % 2]
            return lax.dot_general(
                q, listed(h, 0), (((1,), (1,)), ((), ())), preferred_element_type=jnp.float32
            )

        waiting = [score(h) for h in range(AHEAD)]
        results = []
        for h in range(H):
            scores = waiting.pop(0)
            probs = jnp.exp(scores - jnp.max(scores, axis=-1, keepdims=True))
            total = jnp.sum(probs, axis=-1, keepdims=True)
            if h + AHEAD < H:
                waiting.append(score(h + AHEAD))
            res = jnp.dot(
                probs.astype(jnp.bfloat16), listed(h, width), preferred_element_type=jnp.float32
            )
            results.append(res * (1.0 / total))
            if h % 2:
                both = jnp.where(low, results[h - 1], results[h])
                ctx[:, pl.ds(h // 2 * 2 * HD, 2 * HD)] = both.astype(jnp.bfloat16)

    def feed_forward(s):
        flag = keep[0, s].astype(jnp.float32)
        if s == 0:
            weight_local(1).wait()
            weight_remote(1, partner).wait_recv()
        branch = jnp.dot(ctx[...], wout[...], preferred_element_type=jnp.float32)
        hidden = (xg[s, me].astype(jnp.float32) + flag * branch).astype(jnp.bfloat16)
        n2 = layer_norm(hidden.astype(jnp.float32), gain2).astype(jnp.bfloat16)
        if s == 0:
            for i in (2, 3):
                weight_local(i).wait()
                weight_remote(i, partner).wait_recv()
        acts = []
        for c in range(0, ff, CHUNK):
            upper = jnp.dot(n2, wup[:, c : c + CHUNK], preferred_element_type=jnp.float32)
            acts.append(jax.nn.gelu(upper, approximate=True).astype(jnp.bfloat16))
        act = jnp.concatenate(acts, axis=1)
        down = jnp.dot(act, wdown[...], preferred_element_type=jnp.float32)
        xo[s] = (hidden.astype(jnp.float32) + flag * down).astype(jnp.bfloat16)

        @pl.when(section < sections - 1)
        def _():
            for c in range(PIECES):
                pass_on(s, c).start()

        pltpu.make_async_copy(xo.at[s], out.at[0, s], out_sem.at[s]).start()
        if s == 0:
            forward(1, 0)

    pltpu.make_async_copy(owners_h, owners, small_sem.at[0]).wait()
    pltpu.make_async_copy(keep_h, keep, small_sem.at[1]).wait()
    pl.when(section == 0)(lambda: start_first(0))
    pl.when(section > 0)(lambda: start_passed(0))
    for s in range(micro):
        gather(s)
        if s + 1 < micro:
            pl.when(section > 0)(lambda: start_passed(s + 1))
        attend(s)
        feed_forward(s)

    for s in range(micro):
        pltpu.make_async_copy(xo.at[s], out.at[0, s], out_sem.at[s]).wait()

        @pl.when(section < sections - 1)
        def _():
            for c in range(PIECES):
                pass_on(s, c).wait_send()

        def drain(k, carry):
            for c in range(PIECES):
                clockwise(s, k, c, at_pos(pos - k)).wait_send()
                counter(s, k, c, at_pos(pos + k)).wait_send()
            return carry

        lax.fori_loop(0, half_ring - 1, drain, 0)
        for c, d in order[: PIECES // 2]:
            clockwise(s, half_ring - 1, c, at_pos(pos - half_ring + 1)).wait_send()
            counter(s, half_ring - 1, d, at_pos(pos + half_ring - 1)).wait_send()
    for i in range(4):
        weight_remote(i, core).wait_send()


def per_device(peers, sections, slides, gains, wqkv, wout, wup, wdown, owners, keep):
    micro, rows, width = slides.shape
    owners, keep = jnp.transpose(owners, (2, 0, 1)), jnp.transpose(keep)
    ff = wup.shape[2]
    any_spec = pl.BlockSpec(memory_space=pl.ANY)
    bf16 = jnp.bfloat16
    dma = pltpu.SemaphoreType.DMA
    return pl.pallas_call(
        functools.partial(kernel, peers, sections, micro),
        out_shape=jax.ShapeDtypeStruct((1, micro, rows, width), bf16),
        in_specs=[
            any_spec, pl.BlockSpec(memory_space=pltpu.VMEM),
            any_spec, any_spec, any_spec, any_spec, any_spec, any_spec,
        ],
        out_specs=any_spec,
        scratch_shapes=[
            pltpu.VMEM((micro, peers, rows, width), bf16),
            pltpu.VMEM((peers, rows, 2 * width), bf16),
            pltpu.VMEM((width, 3 * width), bf16),
            pltpu.VMEM((width, width), bf16),
            pltpu.VMEM((width, ff), bf16),
            pltpu.VMEM((ff, width), bf16),
            pltpu.VMEM((rows, width), bf16),
            pltpu.VMEM((rows, width), bf16),
            pltpu.VMEM((micro, rows, width), bf16),
            pltpu.SMEM(owners.shape, jnp.int32),
            pltpu.SMEM(keep.shape, jnp.int32),
            dma((4,)), dma((4,)), dma((4,)),
            dma((micro,)), dma((micro,)), dma((micro, PIECES)), dma((micro, PIECES)),
            dma((micro, peers // 2, PIECES)), dma((micro, peers // 2, PIECES)),
            dma((micro, peers // 2, PIECES)), dma((micro, peers // 2, PIECES)),
            dma((2,)),
        ],
        compiler_params=pltpu.CompilerParams(
            collective_id=0, has_side_effects=True, vmem_limit_bytes=60 * 1024 * 1024
        ),
    )(slides, gains, wqkv, wout, wup, wdown, owners, keep)


def solution(mesh):
    return jax.shard_map(
        functools.partial(per_device, mesh.shape["seq"], mesh.shape["pipe"]),
        mesh=mesh,
        in_specs=(
            P("dp", "seq", None),
            P("pipe", None, None),
            P("pipe", "dp", None),
            P("pipe", "dp", None),
            P("pipe", "dp", None),
            P("pipe", "dp", None),
            P(),
            P("dp", "pipe"),
        ),
        out_specs=P("pipe", "dp", "seq", None),
        check_vma=False,
    )
```

```python
import functools

import jax
import jax.numpy as jnp
from jax import lax
from jax.experimental import pallas as pl
from jax.experimental.pallas import tpu as pltpu
from jax.sharding import PartitionSpec as P

H = 12
HD = 64
BLOCK = 128
PICKS = 3
AHEAD = 3
CHUNK = 512
KV_CHUNK = 1536
PIECES = 4
MESH_ID = pl.DeviceIdType.MESH


def layer_norm(values, gain):
    mean = jnp.mean(values, axis=-1, keepdims=True)
    centred = values - mean
    var = jnp.mean(centred * centred, axis=-1, keepdims=True)
    return centred * lax.rsqrt(var + 1e-05) * gain


def kernel(
    peers, sections, micro, slides, gains, wqkv_h, wout_h, wup_h, wdown_h, owners_h, keep_h, out,
    xg, kv, wqkv, wout, wup, wdown, qbuf, ctx, xo, owners, keep,
    wl_sem, ws_sem, wr_sem, in_sem, out_sem, ps_sem, pr_sem,
    cw_s, cw_r, cc_s, cc_r, small_sem,
):
    width = slides.shape[2]
    ff = wup_h.shape[2]
    half_ring = peers // 2
    core = lax.axis_index("dp")
    section = lax.axis_index("pipe")
    me = lax.axis_index("seq")

    def pos_of(i):
        z, x = i // 2, i % 2
        return z + x * (peers - 1 - 2 * z)

    def at_pos(p):
        p = (p + 2 * peers) % peers
        x = p // half_ring
        return 2 * (p + x * (peers - 1 - 2 * p)) + x

    pos = pos_of(me)
    right, left = at_pos(pos + 1), at_pos(pos - 1)
    partner = 1 - core
    after = (section + 1) % sections
    before = (section + sections - 1) % sections

    def own_copy(s):
        return pltpu.make_async_copy(slides.at[s], xg.at[s, me], in_sem.at[s])

    @pl.when(section == 0)
    def _():
        for s in range(micro):
            own_copy(s).start()

    pltpu.make_async_copy(owners_h, owners, small_sem.at[0]).start()
    pltpu.make_async_copy(keep_h, keep, small_sem.at[1]).start()

    halves = ((wqkv_h, wqkv), (wout_h, wout), (wup_h, wup), (wdown_h, wdown))

    def weight_local(i):
        part, full = halves[i]
        rows = part.shape[1]
        return pltpu.make_async_copy(
            part.at[0], full.at[pl.ds(pl.multiple_of(core * rows, rows), rows)], wl_sem.at[i]
        )

    def weight_remote(i, place):
        part, full = halves[i]
        rows = part.shape[1]
        return pltpu.make_async_remote_copy(
            src_ref=part.at[0],
            dst_ref=full.at[pl.ds(pl.multiple_of(place * rows, rows), rows)],
            send_sem=ws_sem.at[i],
            recv_sem=wr_sem.at[i],
            device_id={"dp": partner},
            device_id_type=MESH_ID,
        )

    for i in range(4):
        weight_local(i).start()

    barrier = pltpu.get_barrier_semaphore()
    for target in (
        {"dp": partner}, {"seq": left}, {"seq": right}, {"pipe": after}, {"pipe": before},
    ):
        pl.semaphore_signal(barrier, inc=1, device_id=target, device_id_type=MESH_ID)
    pl.semaphore_wait(barrier, 5)

    for i in range(4):
        weight_remote(i, core).start()

    rows_of = [pl.ds(c * (BLOCK // PIECES), BLOCK // PIECES) for c in range(PIECES)]

    def clockwise(s, k, c, owner):
        piece = xg.at[s, owner, rows_of[c]]
        return pltpu.make_async_remote_copy(
            src_ref=piece, dst_ref=piece, send_sem=cw_s.at[s, k, c], recv_sem=cw_r.at[s, k, c],
            device_id={"seq": right}, device_id_type=MESH_ID,
        )

    def counter(s, k, c, owner):
        piece = xg.at[s, owner, rows_of[c]]
        return pltpu.make_async_remote_copy(
            src_ref=piece, dst_ref=piece, send_sem=cc_s.at[s, k, c], recv_sem=cc_r.at[s, k, c],
            device_id={"seq": left}, device_id_type=MESH_ID,
        )

    def pass_on(s, c):
        return pltpu.make_async_remote_copy(
            src_ref=xo.at[s, rows_of[c]], dst_ref=xg.at[s, me, rows_of[c]],
            send_sem=ps_sem.at[s, c], recv_sem=pr_sem.at[s, c],
            device_id={"pipe": after}, device_id_type=MESH_ID,
        )

    order = list(zip(range(PIECES), reversed(range(PIECES))))

    def start_first(s):
        own_copy(s).wait()
        for c, d in order:
            clockwise(s, 0, c, me).start()
            counter(s, 0, d, me).start()

    def start_passed(s):
        for c in range(PIECES):
            pass_on(s, c).wait_recv()
            clockwise(s, 0, c, me).start()
            counter(s, 0, c, me).start()

    def forward(s, k):
        a, b = at_pos(pos - k - 1), at_pos(pos + k + 1)
        for i, (c, d) in enumerate(order):
            clockwise(s, k, c, a).wait_recv()
            if i < PIECES // 2:
                clockwise(s, k + 1, c, a).start()
            else:
                pl.when(k < half_ring - 2)(lambda: clockwise(s, k + 1, c, a).start())
            counter(s, k, d, b).wait_recv()
            if i < PIECES // 2:
                counter(s, k + 1, d, b).start()
            else:
                pl.when(k < half_ring - 2)(lambda: counter(s, k + 1, d, b).start())

    def drain_sends(s):
        @pl.when(section < sections - 1)
        def _():
            for c in range(PIECES):
                pass_on(s, c).wait_send()

        def drain(k, carry):
            for c in range(PIECES):
                clockwise(s, k, c, at_pos(pos - k)).wait_send()
                counter(s, k, c, at_pos(pos + k)).wait_send()
            return carry

        lax.fori_loop(0, half_ring - 1, drain, 0)
        for c, d in order[: PIECES // 2]:
            clockwise(s, half_ring - 1, c, at_pos(pos - half_ring + 1)).wait_send()
            counter(s, half_ring - 1, d, at_pos(pos + half_ring - 1)).wait_send()
        if s == 0:
            for i in range(4):
                weight_remote(i, core).wait_send()

    gain1 = gains[0, 0:1, :]
    gain2 = gains[0, 1:2, :]

    def keys_values(blocks, n1):
        for c in range(0, 2 * width, KV_CHUNK):
            part = jnp.dot(
                n1, wqkv[:, width + c : width + c + KV_CHUNK], preferred_element_type=jnp.float32
            ).astype(jnp.bfloat16)
            for b, block in enumerate(blocks):
                kv[block, :, c : c + KV_CHUNK] = part[b * BLOCK : (b + 1) * BLOCK]

    def gather(s):
        n1 = layer_norm(xg[s, me].astype(jnp.float32), gain1).astype(jnp.bfloat16)
        if s == 0:
            weight_local(0).wait()
            weight_remote(0, partner).wait_recv()
        qbuf[...] = jnp.dot(
            n1, wqkv[:, :width], preferred_element_type=jnp.float32
        ).astype(jnp.bfloat16)
        keys_values((me,), n1)

        def step(k, carry):
            if s == 0:
                forward(s, k)
            else:
                pl.when(k >= 1)(lambda: forward(s, k))
            a, b = at_pos(pos - k - 1), at_pos(pos + k + 1)
            both = jnp.concatenate([xg[s, a], xg[s, b]], axis=0).astype(jnp.float32)
            keys_values((a, b), layer_norm(both, gain1).astype(jnp.bfloat16))
            return carry

        lax.fori_loop(0, half_ring - 1, step, 0)
        if s + 1 < micro:
            pl.when(section == 0)(lambda: start_first(s + 1))
        if s > 0:
            drain_sends(s - 1)
        far = at_pos(pos + half_ring)
        for c, d in order[: PIECES // 2]:
            clockwise(s, half_ring - 1, c, far).wait_recv()
            counter(s, half_ring - 1, d, far).wait_recv()
        n1 = layer_norm(xg[s, far].astype(jnp.float32), gain1).astype(jnp.bfloat16)
        keys_values((far,), n1)

    lane = lax.broadcasted_iota(jnp.int32, (1, 2 * HD), 1)
    low = lane < HD
    masks = [
        jnp.where(low, 0.125, 0.0).astype(jnp.bfloat16),
        jnp.where(low, 0.0, 0.125).astype(jnp.bfloat16),
    ]

    def attend(s):
        def listed(h, base):
            cols = pl.ds(base + h // 2 * 2 * HD, 2 * HD)
            blocks = [me] + [owners[i, me, h] for i in range(PICKS)]
            return jnp.concatenate([kv[o, :, cols] for o in blocks], axis=0)

        def score(h):
            q = qbuf[:, pl.ds(h // 2 * 2 * HD, 2 * HD)] * masks[h % 2]
            return lax.dot_general(
                q, listed(h, 0), (((1,), (1,)), ((), ())), preferred_element_type=jnp.float32
            )

        waiting = [score(h) for h in range(AHEAD)]
        results = []
        for h in range(H):
            scores = waiting.pop(0)
            probs = jnp.exp(scores - jnp.max(scores, axis=-1, keepdims=True))
            total = jnp.sum(probs, axis=-1, keepdims=True)
            if h + AHEAD < H:
                waiting.append(score(h + AHEAD))
            res = jnp.dot(
                probs.astype(jnp.bfloat16), listed(h, width), preferred_element_type=jnp.float32
            )
            results.append(res * (1.0 / total))
            if h % 2:
                both = jnp.where(low, results[h - 1], results[h])
                ctx[:, pl.ds(h // 2 * 2 * HD, 2 * HD)] = both.astype(jnp.bfloat16)

    def feed_forward(s):
        flag = keep[0, s].astype(jnp.float32)
        if s == 0:
            weight_local(1).wait()
            weight_remote(1, partner).wait_recv()
        branch = jnp.dot(ctx[...], wout[...], preferred_element_type=jnp.float32)
        hidden = (xg[s, me].astype(jnp.float32) + flag * branch).astype(jnp.bfloat16)
        n2 = layer_norm(hidden.astype(jnp.float32), gain2).astype(jnp.bfloat16)
        if s == 0:
            for i in (2, 3):
                weight_local(i).wait()
                weight_remote(i, partner).wait_recv()
        acts = []
        for c in range(0, ff, CHUNK):
            upper = jnp.dot(n2, wup[:, c : c + CHUNK], preferred_element_type=jnp.float32)
            acts.append(jax.nn.gelu(upper, approximate=True).astype(jnp.bfloat16))
        act = jnp.concatenate(acts, axis=1)
        down = jnp.dot(act, wdown[...], preferred_element_type=jnp.float32)
        xo[s] = (hidden.astype(jnp.float32) + flag * down).astype(jnp.bfloat16)

        @pl.when(section < sections - 1)
        def _():
            for c in range(PIECES):
                pass_on(s, c).start()

        pltpu.make_async_copy(xo.at[s], out.at[0, s], out_sem.at[s]).start()
        if s == 0:
            forward(1, 0)

    pltpu.make_async_copy(owners_h, owners, small_sem.at[0]).wait()
    pltpu.make_async_copy(keep_h, keep, small_sem.at[1]).wait()
    pl.when(section == 0)(lambda: start_first(0))
    pl.when(section > 0)(lambda: start_passed(0))
    for s in range(micro):
        gather(s)
        if s + 1 < micro:
            pl.when(section > 0)(lambda: start_passed(s + 1))
        attend(s)
        feed_forward(s)

    drain_sends(micro - 1)
    for s in range(micro):
        pltpu.make_async_copy(xo.at[s], out.at[0, s], out_sem.at[s]).wait()


def per_device(peers, sections, slides, gains, wqkv, wout, wup, wdown, owners, keep):
    micro, rows, width = slides.shape
    owners, keep = jnp.transpose(owners, (2, 0, 1)), jnp.transpose(keep)
    ff = wup.shape[2]
    any_spec = pl.BlockSpec(memory_space=pl.ANY)
    bf16 = jnp.bfloat16
    dma = pltpu.SemaphoreType.DMA
    return pl.pallas_call(
        functools.partial(kernel, peers, sections, micro),
        out_shape=jax.ShapeDtypeStruct((1, micro, rows, width), bf16),
        in_specs=[
            any_spec, pl.BlockSpec(memory_space=pltpu.VMEM),
            any_spec, any_spec, any_spec, any_spec, any_spec, any_spec,
        ],
        out_specs=any_spec,
        scratch_shapes=[
            pltpu.VMEM((micro, peers, rows, width), bf16),
            pltpu.VMEM((peers, rows, 2 * width), bf16),
            pltpu.VMEM((width, 3 * width), bf16),
            pltpu.VMEM((width, width), bf16),
            pltpu.VMEM((width, ff), bf16),
            pltpu.VMEM((ff, width), bf16),
            pltpu.VMEM((rows, width), bf16),
            pltpu.VMEM((rows, width), bf16),
            pltpu.VMEM((micro, rows, width), bf16),
            pltpu.SMEM(owners.shape, jnp.int32),
            pltpu.SMEM(keep.shape, jnp.int32),
            dma((4,)), dma((4,)), dma((4,)),
            dma((micro,)), dma((micro,)), dma((micro, PIECES)), dma((micro, PIECES)),
            dma((micro, peers // 2, PIECES)), dma((micro, peers // 2, PIECES)),
            dma((micro, peers // 2, PIECES)), dma((micro, peers // 2, PIECES)),
            dma((2,)),
        ],
        compiler_params=pltpu.CompilerParams(
            collective_id=0, has_side_effects=True, vmem_limit_bytes=60 * 1024 * 1024
        ),
    )(slides, gains, wqkv, wout, wup, wdown, owners, keep)


def solution(mesh):
    return jax.shard_map(
        functools.partial(per_device, mesh.shape["seq"], mesh.shape["pipe"]),
        mesh=mesh,
        in_specs=(
            P("dp", "seq", None),
            P("pipe", None, None),
            P("pipe", "dp", None),
            P("pipe", "dp", None),
            P("pipe", "dp", None),
            P("pipe", "dp", None),
            P(),
            P("dp", "pipe"),
        ),
        out_specs=P("pipe", "dp", "seq", None),
        check_vma=False,
    )
```
